128 devices in a mesh: blk: 32 (over z, y, core), grp: 4 (over x).
Axes of the slice: x: 4, y: 4, z: 4, core: 2. Of those that a mesh axis runs over, the one named last changes fastest.
Arguments:
- block_inverse: bfloat16 [256, 1024, 1024], P(('blk', 'grp')), may hold values from -5 to 5
- coupling_in: bfloat16 [256, 1024, 1536], P(('blk', 'grp')), may hold values from -0.046875 to 0.046875
- coupling_out: bfloat16 [256, 1536, 1024], P(('blk', 'grp')), may hold values from -0.15625 to 0.15625
- sensitivities: bfloat16 [256, 1024, 512], P(('blk', 'grp')), may hold values from -6 to 6
- border_rhs: bfloat16 [1536, 512], replicated, may hold values from -6 to 6
- border_inverse: bfloat16 [1536, 1536], P('blk'), may hold values from -5 to 5
Outputs:
- adjoint: bfloat16 [256, 1024, 512], P(('blk', 'grp'))
- border_part: bfloat16 [1536, 512], P('blk')
The draws below stay inside these ranges and needn't reach their ends.
All inputs are finite; a program needn't handle non-finite values.
Results may differ from the reference program's by a relative error of at most 0.0067.
Values may be sent and summed in bfloat16 or wider, within the bound.
No kernel may reach another device: no remote copies, remote signals or barrier semaphores. Data moves between devices by JAX's collectives and lax.ppermute only.
A program may use at most 128 MiB of HBM per device.

```python
import math
import jax
import jax.numpy as jnp
from jax import lax

BLOCK = 1024
LINK = 1536
COLS = 512
NBLOCKS = 256


def dominant_matrix(key, lead_shape, order):
    key_diag, key_off = jax.random.split(key, 2)
    diag_vals = jax.random.uniform(key_diag, lead_shape + (order,), jnp.float32, 0.5, 1.5)
    off_vals = jnp.clip(jax.random.normal(key_off, lead_shape + (order, order), jnp.float32), -4.0, 4.0) * (0.5 / math.sqrt(order))
    matrix = off_vals + jnp.eye(order, dtype=jnp.float32) * diag_vals[..., None, :]
    return matrix


def draw_block_inverse(key, part):
    return dominant_matrix(jax.random.fold_in(key, 11), (NBLOCKS,), BLOCK).astype(jnp.bfloat16)


def draw_border_inverse(key, part):
    return dominant_matrix(jax.random.fold_in(key, 23), (), LINK).astype(jnp.bfloat16)


def spiked(values, key, source, target, shards_of, factor):
    def block_of(dim):
        return (jnp.arange(values.shape[dim]) // (values.shape[dim] // shards_of)).reshape((-1,) + (1,) * (values.ndim - 1 - dim))

    one_side = jax.random.permutation(key, shards_of)[block_of(target)]
    other_side = (block_of(target) + shards_of // 2) % shards_of
    return jnp.where((block_of(source) == one_side) | (block_of(source) == other_side), factor * values, values)


def level_of(own_key, shape, pieces, smallest, largest):
    def one(dim, blocks):
        draws = jax.random.uniform(jax.random.fold_in(jax.random.fold_in(own_key, 6), dim), (blocks,), jnp.float32, smallest / len(pieces), largest / len(pieces))
        return jnp.repeat(jnp.exp(draws), shape[dim] // blocks).reshape((-1,) + (1,) * (len(shape) - dim - 1))

    gain = one(*pieces[0])
    for cut in pieces[1:]:
        gain = gain * one(*cut)
    return gain


def centred(key, shape, deviation, bound, cuts=(), kind=jnp.bfloat16):
    level = level_of(key, shape, cuts, -0.22, 0.18) if cuts else 1.0
    array = jax.random.normal(key, shape, jnp.float32) * deviation * level
    return jnp.minimum(jnp.maximum(array, -bound), bound).astype(kind)


def noise_with(key, shape, spread, limit, shards, heavy, kind=jnp.bfloat16):
    result = spread * jax.random.normal(key, shape, jnp.float32)
    if shards:
        result = result * level_of(key, shape, shards, -0.22, 0.18)
    return jnp.clip(spiked(result, jax.random.fold_in(key, 3), *heavy), -limit, limit).astype(kind)


def setup_inputs(seed: int = 0) -> dict:
    key_list = jax.random.split(jax.random.key(seed), 7)
    block_inverse = draw_block_inverse(jax.random.fold_in(key_list[6], 71), 0)
    coupling_in = noise_with(key_list[1], (NBLOCKS, BLOCK, LINK), (BLOCK * NBLOCKS) ** -0.5, 0.046875, ((0, 128),), (0, 2, 128, 5.5))
    coupling_out = centred(key_list[2], (NBLOCKS, LINK, BLOCK), LINK ** -0.5, 0.15625, ((0, 128),))
    sensitivities = centred(key_list[3], (NBLOCKS, BLOCK, COLS), 1.0, 6.0, ((0, 128),))
    border_rhs = centred(key_list[4], (LINK, COLS), 1.0, 6.0)
    border_inverse = draw_border_inverse(jax.random.fold_in(key_list[6], 71), 0)
    return dict(block_inverse=block_inverse, coupling_in=coupling_in, coupling_out=coupling_out, sensitivities=sensitivities, border_rhs=border_rhs, border_inverse=border_inverse)


def reference(block_inverse, coupling_in, coupling_out, sensitivities, border_rhs, border_inverse):
    def first_pass(running, blocks):
        inverse_block, couple_block, sens_block = blocks
        forward_block = jnp.dot(inverse_block.T, sens_block, preferred_element_type=jnp.float32)
        forward_half = forward_block.astype(jnp.bfloat16)
        running = running + jnp.dot(couple_block.T, forward_half, preferred_element_type=jnp.float32)
        return running, forward_block

    start_sum = jnp.zeros((LINK, COLS), jnp.float32)
    summed, forward_part = lax.scan(first_pass, start_sum, (block_inverse, coupling_in, sensitivities))
    residual = border_rhs.astype(jnp.float32) - summed
    residual_half = residual.astype(jnp.bfloat16)
    border_part = jnp.dot(border_inverse.T, residual_half, preferred_element_type=jnp.float32).astype(jnp.bfloat16)

    def second_pass(blocks):
        inverse_block, couple_block, forward_block = blocks
        pulled = jnp.dot(couple_block.T, border_part, preferred_element_type=jnp.float32).astype(jnp.bfloat16)
        back_term = jnp.dot(inverse_block.T, pulled, preferred_element_type=jnp.float32)
        return (forward_block - back_term).astype(jnp.bfloat16)

    adjoint = lax.map(second_pass, (block_inverse, coupling_out, forward_part))
    return adjoint, border_part
```

```python
import jax
import jax.numpy as jnp
from jax import lax
from jax.sharding import Mesh, PartitionSpec as P

F32 = jnp.float32
BF16 = jnp.bfloat16
CHIPS = ("z", "y", "xh", "xl")
SWAP = [(0, 1), (1, 0)]


def body(block_inverse, coupling_in, coupling_out, sensitivities, border_rhs, border_inverse):
    core = lax.axis_index("core")
    xl = lax.axis_index("xl")
    chip = lax.axis_index(CHIPS)
    blk = lax.axis_index(("z", "y", "core"))
    rows, link = border_inverse.shape
    cols = sensitivities.shape[2]
    half, quarter = link // 2, link // 4
    piece = cols // 64

    chunks = border_inverse.reshape(rows, 2, 2, quarter)
    chunks = lax.dynamic_index_in_dim(chunks, xl, 2, keepdims=False).swapaxes(0, 1)
    chunks = jnp.broadcast_to(chunks[None], (16, 2, rows, quarter)).reshape(32, rows, quarter)
    solve_cols = lax.all_to_all(chunks, ("z", "y", "core"), 0, 0, tiled=True).reshape(link, quarter)

    forward = jnp.einsum("bjk,bji->bki", sensitivities, block_inverse, preferred_element_type=F32)
    forward, = lax.optimization_barrier((forward,))
    term = jnp.einsum("bkn,bnm->km", forward.astype(BF16), coupling_in, preferred_element_type=F32)

    away = lax.dynamic_slice_in_dim(term, (1 - core) * half, half, 1).astype(BF16)
    mine = lax.dynamic_slice_in_dim(term, core * half, half, 1)
    mine = (mine + lax.ppermute(away, "core", SWAP).astype(F32)).astype(BF16)
    parts = lax.all_to_all(mine.reshape(64, piece, half), CHIPS, 0, 0, tiled=True)
    total = jnp.sum(parts.astype(F32), axis=0)

    pick = (lax.broadcasted_iota(jnp.int32, (piece, cols), 1) == chip * piece + lax.broadcasted_iota(jnp.int32, (piece, cols), 0)).astype(BF16)
    rhs_half = lax.dynamic_slice_in_dim(border_rhs, core * half, half, 0)
    rhs = lax.dot_general(pick, rhs_half, (((1,), (1,)), ((), ())), preferred_element_type=F32)
    residual = (rhs - total).astype(BF16)
    other = lax.ppermute(residual, "xl", SWAP)
    residual = jnp.where(xl == 0, jnp.concatenate([residual, other], 0), jnp.concatenate([other, residual], 0))
    other = lax.ppermute(residual, "core", SWAP)
    residual = jnp.where(core == 0, jnp.concatenate([residual, other], 1), jnp.concatenate([other, residual], 1))

    solved = jnp.dot(residual, solve_cols, preferred_element_type=F32).astype(BF16)
    spread = jnp.broadcast_to(solved[None], (64,) + solved.shape)
    got = lax.all_to_all(spread, CHIPS, 0, 0, tiled=True)
    own = got.reshape(32, 2, 2 * piece, quarter).swapaxes(1, 2).reshape(cols, half)
    other = lax.ppermute(own, "core", SWAP)
    border = jnp.where(core == 0, jnp.concatenate([own, other], 1), jnp.concatenate([other, own], 1))

    pulled = jnp.einsum("km,bmn->bkn", border, coupling_out, preferred_element_type=F32).astype(BF16)
    pulled, = lax.optimization_barrier((pulled,))
    back = jnp.einsum("bkj,bji->bki", pulled, block_inverse, preferred_element_type=F32)
    adjoint = (forward - back).astype(BF16)
    adjoint, = lax.optimization_barrier((adjoint,))
    adjoint = adjoint.swapaxes(1, 2)

    pick = (lax.broadcasted_iota(jnp.int32, (rows, link), 1) == blk * rows + lax.broadcasted_iota(jnp.int32, (rows, link), 0)).astype(BF16)
    border_rows = lax.dot_general(pick, border, (((1,), (1,)), ((), ())), preferred_element_type=F32).astype(BF16)
    return (adjoint, border_rows)


def solution(mesh):
    mesh = Mesh(mesh.devices.reshape(4, 4, 2, 2, 2), ("z", "y", "core", "xh", "xl"))
    every = ("z", "y", "core", "xh", "xl")
    blocks = P(every, None, None)
    lines = P(("z", "y", "core"), None)
    return jax.shard_map(
        body, mesh=mesh, in_specs=(blocks, blocks, blocks, blocks, P(), lines), out_specs=(blocks, lines), check_vma=False
    )
```

```python
import jax
import jax.numpy as jnp
from jax import lax
from jax.experimental import pallas as pl
from jax.experimental.pallas import tpu as pltpu
from jax.sharding import Mesh, PartitionSpec as P

F32 = jnp.float32
BF16 = jnp.bfloat16
CHIPS = ("z", "y", "xh", "xl")
SWAP = [(0, 1), (1, 0)]
HBM = pl.BlockSpec(memory_space=pltpu.HBM)
VMEM = pl.BlockSpec(memory_space=pltpu.VMEM)


def params(mib):
    return pltpu.CompilerParams(vmem_limit_bytes=mib << 20)


def dot(a, b):
    return jnp.dot(a, b, preferred_element_type=F32)


def front_kernel(sens_hbm, inv_hbm, coup_hbm, fwd_hbm, fwd_half, away, coup_mine, fwd, inv, sens, coup_away, sems, out_sems):
    half = away.shape[1]
    core = lax.axis_index("core")
    copies = []
    for b in range(2):
        copies.append(pltpu.make_async_copy(sens_hbm.at[b], sens.at[b], sems.at[len(copies)]))
        copies.append(pltpu.make_async_copy(inv_hbm.at[b], inv.at[b], sems.at[len(copies)]))
    for b in range(2):
        lanes = pl.ds(pl.multiple_of((1 - core) * half, 128), half)
        copies.append(pltpu.make_async_copy(coup_hbm.at[b, :, lanes], coup_away.at[b], sems.at[len(copies)]))
    for b in range(2):
        lanes = pl.ds(pl.multiple_of(core * half, 128), half)
        copies.append(pltpu.make_async_copy(coup_hbm.at[b, :, lanes], coup_mine.at[b], sems.at[len(copies)]))
    outs = [pltpu.make_async_copy(fwd.at[b], fwd_hbm.at[b], out_sems.at[b]) for b in range(2)]
    for copy in copies:
        copy.start()
    for b in range(2):
        copies[2 * b].wait()
        turned = sens[b].T
        copies[2 * b + 1].wait()
        value = dot(turned, inv[b])
        fwd[b] = value
        outs[b].start()
        fwd_half[b] = value.astype(BF16)
    copies[4].wait()
    copies[5].wait()
    away[...] = (dot(fwd_half[0], coup_away[0]) + dot(fwd_half[1], coup_away[1])).astype(BF16)
    copies[6].wait()
    copies[7].wait()
    outs[0].wait()
    outs[1].wait()


def front(sens, inv, coup):
    n, k, m = inv.shape[1], sens.shape[2], coup.shape[2]
    return pl.pallas_call(
        front_kernel,
        name="front",
        out_shape=(
            pltpu.HBM((2, k, n), F32),
            pltpu.VMEM((2, k, n), BF16),
            pltpu.VMEM((k, m // 2), BF16),
            pltpu.VMEM((2, n, m // 2), BF16),
        ),
        in_specs=[HBM] * 3,
        out_specs=[HBM] + [VMEM] * 3,
        scratch_shapes=[
            pltpu.VMEM((2, k, n), F32),
            pltpu.VMEM((2, n, n), BF16),
            pltpu.VMEM((2, n, k), BF16),
            pltpu.VMEM((2, n, m // 2), BF16),
            pltpu.SemaphoreType.DMA((8,)),
            pltpu.SemaphoreType.DMA((2,)),
        ],
        compiler_params=params(30),
        cost_estimate=pl.CostEstimate(flops=2 * 2 * n * k * (n + m // 2), bytes_accessed=13 << 20, transcendentals=0),
    )(hb(sens), hb(inv), hb(coup))


def mine_kernel(fwd_half, coup_mine, out):
    out[...] = dot(fwd_half[0], coup_mine[0]) + dot(fwd_half[1], coup_mine[1])


def mine_half(fwd_half, coup_mine):
    k, m = fwd_half.shape[1], coup_mine.shape[2]
    return pl.pallas_call(
        mine_kernel,
        name="mine",
        out_shape=pltpu.VMEM((k, m), F32),
        in_specs=[VMEM] * 2,
        out_specs=VMEM,
        compiler_params=params(8),
        cost_estimate=pl.CostEstimate(flops=4 * k * m * fwd_half.shape[2], bytes_accessed=6 << 20, transcendentals=0),
    )(vm(fwd_half), vm(coup_mine))


def vm(x):
    return pltpu.with_memory_space_constraint(x, pltpu.VMEM)


def hb(x):
    return pltpu.with_memory_space_constraint(x, pltpu.HBM)


def pull_own_kernel(got, coup_hbm, out, coup_other, coup, sems):
    quarter = got.shape[3]
    half = 2 * quarter
    core = lax.axis_index("core")
    own = pl.ds(pl.multiple_of(core * half, 128), half)
    far = pl.ds(pl.multiple_of((1 - core) * half, 128), half)
    copies = [pltpu.make_async_copy(coup_hbm.at[b, own, :], coup.at[b], sems.at[b]) for b in range(2)]
    copies += [pltpu.make_async_copy(coup_hbm.at[b, far, :], coup_other.at[b], sems.at[2 + b]) for b in range(2)]
    for copy in copies:
        copy.start()
    lhs = [got[:, q].reshape(-1, quarter) for q in range(2)]
    for b in range(2):
        copies[b].wait()
        out[b] = dot(lhs[0], coup[b, :quarter, :]) + dot(lhs[1], coup[b, quarter:, :])
    copies[2].wait()
    copies[3].wait()


def pull_own(got, coup):
    k, m, n = got.shape[0] * got.shape[2], coup.shape[1], coup.shape[2]
    return pl.pallas_call(
        pull_own_kernel,
        name="pull_own",
        out_shape=(pltpu.VMEM((2, k, n), F32), pltpu.VMEM((2, m // 2, n), BF16)),
        in_specs=[VMEM, HBM],
        out_specs=[VMEM] * 2,
        scratch_shapes=[pltpu.VMEM((2, m // 2, n), BF16), pltpu.SemaphoreType.DMA((4,))],
        compiler_params=params(16),
        cost_estimate=pl.CostEstimate(flops=2 * k * n * m, bytes_accessed=8 << 20, transcendentals=0),
    )(vm(got), hb(coup))


def back_kernel(own, other, part, coup, inv_hbm, fwd_hbm, adjoint_hbm, border_hbm, inv, fwd, adjoint, border, sems):
    quarter = own.shape[3]
    core = lax.axis_index("core")
    zed = lax.axis_index("z")
    loads = []
    for b in range(2):
        loads.append(pltpu.make_async_copy(inv_hbm.at[b], inv.at[b], sems.at[3 + 2 * b]))
        loads.append(pltpu.make_async_copy(fwd_hbm.at[b], fwd.at[b], sems.at[4 + 2 * b]))
    for copy in loads:
        copy.start()
    lhs = [other[:, q].reshape(-1, quarter) for q in range(2)]
    copies = [pltpu.make_async_copy(adjoint.at[b], adjoint_hbm.at[b], sems.at[b]) for b in range(2)]
    copies.append(pltpu.make_async_copy(border, border_hbm, sems.at[2]))

    rows = border.shape[0]
    first = (lax.axis_index("y") * 2 + core) * rows
    spot = first + lax.broadcasted_iota(jnp.int32, (rows, quarter), 0)
    pick = (lax.broadcasted_iota(jnp.int32, (rows, quarter), 1) == spot).astype(BF16)

    def choose(ref):
        picked = ref[:, pl.ds(lax.rem(zed, 2), 1)].reshape(-1, quarter)
        border[...] = lax.dot_general(pick, picked, (((1,), (1,)), ((), ())), preferred_element_type=F32).astype(BF16)

    @pl.when(zed // 2 == core)
    def _():
        choose(own)

    @pl.when(zed // 2 != core)
    def _():
        choose(other)

    copies[2].start()
    for b in range(2):
        pulled = part[b] + dot(lhs[0], coup[b, :quarter, :]) + dot(lhs[1], coup[b, quarter:, :])
        loads[2 * b].wait()
        value = dot(pulled.astype(BF16), inv[b])
        loads[2 * b + 1].wait()
        adjoint[b] = (fwd[b] - value).astype(BF16).T
        copies[b].start()
    for copy in copies:
        copy.wait()


def backward(own, other, part, coup, inv, fwd, rows):
    _, k, n = part.shape
    return pl.pallas_call(
        back_kernel,
        name="back",
        out_shape=(jax.ShapeDtypeStruct((2, n, k), BF16), jax.ShapeDtypeStruct((rows, k), BF16)),
        in_specs=[VMEM] * 4 + [HBM] * 2,
        out_specs=[HBM] * 2,
        scratch_shapes=[
            pltpu.VMEM((2, n, n), BF16),
            pltpu.VMEM((2, k, n), F32),
            pltpu.VMEM((2, n, k), BF16),
            pltpu.VMEM((rows, k), BF16),
            pltpu.SemaphoreType.DMA((7,)),
        ],
        compiler_params=params(24),
        cost_estimate=pl.CostEstimate(flops=4 * k * n * (n + coup.shape[1]), bytes_accessed=20 << 20, transcendentals=0),
    )(vm(own), vm(other), vm(part), vm(coup), hb(inv), hb(fwd))


def steps(block_inverse, coupling_in, coupling_out, sensitivities, border_rhs, border_inverse):
    core = lax.axis_index("core")
    xl = lax.axis_index("xl")
    chip = lax.axis_index(CHIPS)
    rows, link = border_inverse.shape
    cols = sensitivities.shape[2]
    half, quarter = link // 2, link // 4
    piece = cols // 64

    chunks = jnp.where(xl == 0,
        jnp.stack([border_inverse[:, :quarter], border_inverse[:, 2 * quarter:3 * quarter]]),
        jnp.stack([border_inverse[:, quarter:2 * quarter], border_inverse[:, 3 * quarter:]]))
    chunks = jnp.broadcast_to(chunks[None], (16, 2, rows, quarter)).reshape(32, rows, quarter)
    solve_cols = lax.all_to_all(chunks, ("z", "y", "core"), 0, 0, tiled=True).reshape(link, quarter)

    fwd, fwd_half, away, coup_mine = front(sensitivities, block_inverse, coupling_in)
    came = lax.ppermute(away, "core", SWAP)
    mine = mine_half(fwd_half, coup_mine)
    mine = (mine + came.astype(F32)).astype(BF16)
    parts = lax.all_to_all(mine.reshape(64, piece, half), CHIPS, 0, 0, tiled=True)
    total = jnp.sum(parts.astype(F32), axis=0)

    pick = (lax.broadcasted_iota(jnp.int32, (piece, cols), 1) == chip * piece + lax.broadcasted_iota(jnp.int32, (piece, cols), 0)).astype(BF16)
    rhs_half = lax.dynamic_slice_in_dim(border_rhs, core * half, half, 0)
    rhs = lax.dot_general(pick, rhs_half, (((1,), (1,)), ((), ())), preferred_element_type=F32)
    residual = (rhs - total).astype(BF16)
    other = lax.ppermute(residual, "xl", SWAP)
    residual = jnp.where(xl == 0, jnp.concatenate([residual, other], 0), jnp.concatenate([other, residual], 0))
    other = lax.ppermute(residual, "core", SWAP)
    residual = jnp.where(core == 0, jnp.concatenate([residual, other], 1), jnp.concatenate([other, residual], 1))

    solved = dot(residual, solve_cols).astype(BF16)
    spread = jnp.broadcast_to(solved[None], (64,) + solved.shape)
    got = lax.all_to_all(spread, CHIPS, 0, 0, tiled=True)
    own = got.reshape(32, 2, 2 * piece, quarter)
    other = lax.ppermute(got, "core", SWAP).reshape(own.shape)
    part, coup_other = pull_own(own, coupling_out)
    return backward(own, other, part, coup_other, block_inverse, fwd, rows)


def solution(mesh):
    mesh = Mesh(mesh.devices.reshape(4, 4, 2, 2, 2), ("z", "y", "core", "xh", "xl"))
    every = ("z", "y", "core", "xh", "xl")
    blocks = P(every, None, None)
    lines = P(("z", "y", "core"), None)
    return jax.shard_map(
        steps, mesh=mesh, in_specs=(blocks, blocks, blocks, blocks, P(), lines), out_specs=(blocks, lines), check_vma=False
    )
```

```python
import jax
import jax.numpy as jnp
from jax import lax
from jax.experimental import pallas as pl
from jax.experimental.pallas import tpu as pltpu
from jax.sharding import Mesh, PartitionSpec as P

F32 = jnp.float32
BF16 = jnp.bfloat16
CHIPS = ("z", "y", "xh", "xl")
SWAP = [(0, 1), (1, 0)]
NEAR = [(0, 1), (1, 0), (2, 3), (3, 2)]
FAR = [(0, 3), (3, 0), (1, 2), (2, 1)]
ORDER = (0, 2, 3, 1)
HBM = pl.BlockSpec(memory_space=pltpu.HBM)
VMEM = pl.BlockSpec(memory_space=pltpu.VMEM)


def call(kernel, outs, ins, operands, scratch=(), mib=16, flops=0, mbytes=1, alias={}):
    return pl.pallas_call(
        kernel,
        out_shape=outs,
        in_specs=ins,
        out_specs=[VMEM if str(o.memory_space) == "vmem" else HBM for o in outs],
        scratch_shapes=list(scratch),
        input_output_aliases=alias,
        compiler_params=pltpu.CompilerParams(vmem_limit_bytes=mib << 20),
        cost_estimate=pl.CostEstimate(flops=flops, bytes_accessed=mbytes << 20, transcendentals=0),
    )(*[pltpu.with_memory_space_constraint(x, s.memory_space) for x, s in zip(operands, ins)])


def dot(a, b):
    return jnp.dot(a, b, preferred_element_type=F32)


def lanes(index, size):
    return pl.ds(pl.multiple_of(index * size, 128), size)


def forward_kernel(sens_hbm, inv_hbm, coup_hbm, fwd_hbm, fwd, away, coup0, coup1, inv, sens, turned, sems):
    half = away.shape[0]
    core = lax.axis_index("core")
    loads = []
    for b in range(2):
        loads.append(pltpu.make_async_copy(sens_hbm.at[b], sens.at[b], sems.at[2 * b]))
        loads.append(pltpu.make_async_copy(inv_hbm.at[b], inv.at[b], sems.at[2 * b + 1]))
    coup = (coup0, coup1)
    loads += [pltpu.make_async_copy(coup_hbm.at[b], coup[b], sems.at[4 + b]) for b in range(2)]
    stores = [pltpu.make_async_copy(fwd.at[b], fwd_hbm.at[b], sems.at[6 + b]) for b in range(2)]
    for load in loads:
        load.start()
    for b in range(2):
        loads[2 * b].wait()
        turned[b] = sens[b].T
        loads[2 * b + 1].wait()
        fwd[b] = dot(turned[b], inv[b]).astype(BF16)
        stores[b].start()
    loads[4].wait()
    total = dot(fwd[0, lanes(1 - core, half), :], coup0[...])
    loads[5].wait()
    away[...] = (total + dot(fwd[1, lanes(1 - core, half), :], coup1[...])).astype(BF16)
    for store in stores:
        store.wait()


def mine_kernel(fwd, coup0, coup1, out):
    half = out.shape[0]
    core = lax.axis_index("core")
    out[...] = dot(fwd[0, lanes(core, half), :], coup0[...]) + dot(fwd[1, lanes(core, half), :], coup1[...])


def order_kernel(ring0, ring1, ring2, ring3, out):
    yed = lax.axis_index("y")
    for step, ring in enumerate((ring0, ring1, ring2, ring3)):
        out[lax.rem(yed + 4 - step, 4)] = ring[...]


def join_kernel(mine, came, out_hbm, out, sems):
    quarter = out.shape[2]
    copies = []
    for z in range(4):
        span = slice(z * quarter, (z + 1) * quarter)
        value = (mine[:, span] + came[:, span].astype(F32)).astype(BF16)
        out[z * 16:(z + 1) * 16] = value.reshape(16, -1, quarter)
        copies.append(pltpu.make_async_copy(out.at[z * 16:(z + 1) * 16], out_hbm.at[z * 16:(z + 1) * 16], sems.at[z]))
        copies[-1].start()
    for copy in copies:
        copy.wait()


def unroll(got, lhs):
    quarter = got.shape[2]
    for z in range(4):
        lhs[:, ORDER[z] * quarter:(ORDER[z] + 1) * quarter] = got[z * 16:(z + 1) * 16].reshape(-1, quarter)


def finish(b, pulled, inv, fwd, adjoint, adjoint_hbm, sems, columns):
    stores = []
    step = inv.shape[2] // 4
    for i in range(4):
        span = slice(i * step, (i + 1) * step)
        value = fwd[b, :, span].astype(F32) - dot(pulled[b], inv[b, :, span])
        adjoint[b, span, :] = value.astype(BF16).T
        stores.append(pltpu.make_async_copy(adjoint.at[b, span, :], adjoint_hbm.at[b, span, columns], sems.at[4 * b + i]))
        stores[-1].start()
    return stores


def own_kernel(got, coup_hbm, inv_hbm, fwd_hbm, adjoint_hbm, coup, inv, fwd, adjoint, lhs, pulled, sems, out_sems):
    half = lhs.shape[0]
    core = lax.axis_index("core")
    third = coup.shape[1] // 3
    loads = []
    for b in range(2):
        for i in range(3):
            span = slice(i * third, (i + 1) * third)
            loads.append(pltpu.make_async_copy(coup_hbm.at[b, span, :], coup.at[b, span, :], sems.at[5 * b + i]))
        loads.append(pltpu.make_async_copy(inv_hbm.at[b], inv.at[b], sems.at[5 * b + 3]))
        loads.append(pltpu.make_async_copy(fwd_hbm.at[b, lanes(core, half), :], fwd.at[b], sems.at[5 * b + 4]))
    for load in loads:
        load.start()
    unroll(got, lhs)
    stores = []
    for b in range(2):
        total = None
        for i in range(3):
            span = slice(i * third, (i + 1) * third)
            loads[5 * b + i].wait()
            value = dot(lhs[:, span], coup[b, span, :])
            total = value if total is None else total + value
        pulled[b] = total.astype(BF16)
        loads[5 * b + 3].wait()
        loads[5 * b + 4].wait()
        stores += finish(b, pulled, inv, fwd, adjoint, adjoint_hbm, out_sems, lanes(core, half))
    for store in stores:
        store.wait()


def other_kernel(own, other, coup, inv, fwd_hbm, _, adjoint_hbm, border_hbm, fwd, adjoint, border, lhs, pulled, sems, out_sems):
    half, quarter = lhs.shape[0], own.shape[2]
    core = lax.axis_index("core")
    zed = lax.axis_index("z")
    loads = [pltpu.make_async_copy(fwd_hbm.at[b, lanes(1 - core, half), :], fwd.at[b], sems.at[b]) for b in range(2)]
    for load in loads:
        load.start()
    unroll(other, lhs)
    stores = []
    for b in range(2):
        pulled[b] = dot(lhs[...], coup[b]).astype(BF16)
        loads[b].wait()
        stores += finish(b, pulled, inv, fwd, adjoint, adjoint_hbm, out_sems, lanes(1 - core, half))
        if b == 0:
            rows = border.shape[0]
            first = (lax.axis_index("y") * 2 + core) * rows
            spot = first + lax.broadcasted_iota(jnp.int32, (rows, quarter), 0)
            pick = (lax.broadcasted_iota(jnp.int32, (rows, quarter), 1) == spot).astype(BF16)
            source = jnp.where(zed == 0, 0, jnp.where(zed == 1, 3, zed - 1))
            for ref, side in ((own, core), (other, 1 - core)):
                chosen = ref[pl.ds(source * 16, 16)].reshape(-1, quarter)
                picked = lax.dot_general(pick, chosen, (((1,), (1,)), ((), ())), preferred_element_type=F32)
                border[:, lanes(side, half)] = picked.astype(BF16)
            stores.append(pltpu.make_async_copy(border, border_hbm, sems.at[2]))
            stores[-1].start()
    for store in stores:
        store.wait()


def steps(block_inverse, coupling_in, coupling_out, sensitivities, border_rhs, border_inverse):
    core = lax.axis_index("core")
    zed = lax.axis_index("z")
    rows, link = border_inverse.shape
    n, cols = sensitivities.shape[1:]
    half, quarter = cols // 2, link // 4
    piece = cols // 32
    sem = pltpu.SemaphoreType.DMA

    ring = [border_inverse]
    for step in (1, 2, 3):
        ring.append(lax.ppermute(border_inverse, "y", [(i, (i + step) % 4) for i in range(4)]))
    ring, = call(order_kernel, (pltpu.VMEM((4, rows, link), BF16),), [VMEM] * 4, ring, (), 2)
    other = lax.ppermute(ring, "core", SWAP)
    plane = jnp.where(core == 0, jnp.stack([ring, other], 1), jnp.stack([other, ring], 1)).reshape(quarter, link)

    fwd, fwd_near, away, coup0, coup1 = call(
        forward_kernel,
        (pltpu.HBM((2, cols, n), BF16), pltpu.VMEM((2, cols, n), BF16), pltpu.VMEM((half, link), BF16)) + (pltpu.VMEM((n, link), BF16),) * 2,
        [HBM] * 3, (sensitivities, block_inverse, coupling_in),
        [pltpu.VMEM((2, n, n), BF16), pltpu.VMEM((2, n, cols), BF16), pltpu.VMEM((2, cols, n), BF16), sem((8,))],
        24, 4 * n * cols * (n + link // 2), 17)
    came = lax.ppermute(away, "core", SWAP)
    mine, = call(mine_kernel, (pltpu.VMEM((half, link), F32),), [VMEM] * 3, (fwd_near, coup0, coup1), (), 8, 4 * n * half * link, 9)
    terms, = call(
        join_kernel, (pltpu.HBM((64, piece, quarter), BF16),), [VMEM] * 2, (mine, came),
        [pltpu.VMEM((64, piece, quarter), BF16), sem((4,))], 4, 0, 3)
    parts = lax.all_to_all(terms, CHIPS, 0, 0, tiled=True)
    total = jnp.sum(parts.astype(F32), axis=0)

    start = core * half + lax.axis_index(("y", "xh", "xl")) * piece
    pick = (lax.broadcasted_iota(jnp.int32, (piece, cols), 1) == start + lax.broadcasted_iota(jnp.int32, (piece, cols), 0)).astype(BF16)
    rhs_part = lax.dynamic_slice_in_dim(border_rhs, zed * quarter, quarter, 0)
    rhs = lax.dot_general(pick, rhs_part, (((1,), (1,)), ((), ())), preferred_element_type=F32)
    residual = (rhs - total).astype(BF16)
    share = dot(residual, plane)
    inner = ((zed == 1) | (zed == 2)).astype(jnp.int32)
    outer = zed // 2
    came = lax.ppermute(lax.dynamic_slice_in_dim(share, (1 - inner) * 2 * quarter, 2 * quarter, 1), "z", NEAR)
    share = lax.dynamic_slice_in_dim(share, inner * 2 * quarter, 2 * quarter, 1) + came
    came = lax.ppermute(lax.dynamic_slice_in_dim(share, (1 - outer) * quarter, quarter, 1), "z", FAR)
    solved = (lax.dynamic_slice_in_dim(share, outer * quarter, quarter, 1) + came).astype(BF16)

    spread = jnp.broadcast_to(solved[None], (64,) + solved.shape)
    own = lax.all_to_all(spread, CHIPS, 0, 0, tiled=True)
    other = lax.ppermute(own, "core", SWAP)

    buffers = [pltpu.VMEM((2, half, n), BF16), pltpu.VMEM((2, n, half), BF16)]
    more = [pltpu.VMEM((half, link), BF16), pltpu.VMEM((2, half, n), BF16)]
    adjoint, coup, inv = call(
        own_kernel, (pltpu.HBM((2, n, cols), BF16), pltpu.VMEM((2, link, n), BF16), pltpu.VMEM((2, n, n), BF16)),
        [VMEM] + [HBM] * 3, (own, coupling_out, block_inverse, fwd), buffers + more + [sem((10,)), sem((8,))],
        12, 4 * half * n * (n + link), 14)
    return call(
        other_kernel, (pltpu.HBM((2, n, cols), BF16), pltpu.HBM((rows, cols), BF16)), [VMEM] * 4 + [HBM] * 2,
        (own, other, coup, inv, fwd, adjoint), buffers + [pltpu.VMEM((rows, cols), BF16)] + more + [sem((3,)), sem((8,))],
        12, 4 * half * n * (n + link), 14, {5: 0})


def body(*args):
    return tuple(steps(*args))


def solution(mesh):
    mesh = Mesh(mesh.devices.reshape(4, 4, 2, 2, 2), ("z", "y", "core", "xh", "xl"))
    every = ("z", "y", "core", "xh", "xl")
    blocks = P(every, None, None)
    lines = P(("z", "y", "core"), None)
    return jax.shard_map(
        body, mesh=mesh, in_specs=(blocks, blocks, blocks, blocks, P(), lines), out_specs=(blocks, lines), check_vma=False
    )
```

```python
import jax
import jax.numpy as jnp
from jax import lax
from jax.experimental import pallas as pl
from jax.experimental.pallas import tpu as pltpu
from jax.sharding import Mesh, PartitionSpec as P

F32 = jnp.float32
BF16 = jnp.bfloat16
CHIPS = ("z", "y", "xh", "xl")
SWAP = [(0, 1), (1, 0)]
NEAR = [(0, 1), (1, 0), (2, 3), (3, 2)]
FAR = [(0, 3), (3, 0), (1, 2), (2, 1)]
ORDER = (0, 2, 3, 1)
HBM = pl.BlockSpec(memory_space=pltpu.HBM)
VMEM = pl.BlockSpec(memory_space=pltpu.VMEM)


def call(kernel, outs, ins, operands, scratch=(), mib=16, flops=0, mbytes=1, alias={}):
    return pl.pallas_call(
        kernel,
        out_shape=outs,
        in_specs=ins,
        out_specs=[VMEM if str(o.memory_space) == "vmem" else HBM for o in outs],
        scratch_shapes=list(scratch),
        input_output_aliases=alias,
        compiler_params=pltpu.CompilerParams(vmem_limit_bytes=mib << 20),
        cost_estimate=pl.CostEstimate(flops=flops, bytes_accessed=mbytes << 20, transcendentals=0),
    )(*[pltpu.with_memory_space_constraint(x, s.memory_space) for x, s in zip(operands, ins)])


def dot(a, b):
    return jnp.dot(a, b, preferred_element_type=F32)


def lanes(index, size):
    return pl.ds(pl.multiple_of(index * size, 128), size)


def forward_kernel(sens_hbm, inv_hbm, coup_hbm, fwd_hbm, fwd1, away, part, coup1, inv, sens, turned, coup0, fwd0, term, sems):
    half = away.shape[0]
    core = lax.axis_index("core")
    fwd = (fwd0, fwd1)
    wide = inv.shape[2] // 2
    columns = [slice(0, wide), slice(wide, 2 * wide)]
    sens_loads = [pltpu.make_async_copy(sens_hbm.at[b], sens.at[b], sems.at[b]) for b in range(2)]
    inv_loads = [[pltpu.make_async_copy(inv_hbm.at[b, :, s], inv.at[b, :, s], sems.at[2 + 2 * b + i]) for i, s in enumerate(columns)] for b in range(2)]
    coup_loads = [pltpu.make_async_copy(coup_hbm.at[b], coup, sems.at[6 + b]) for b, coup in enumerate((coup0, coup1))]
    for load in (sens_loads[0], *inv_loads[0], coup_loads[0], sens_loads[1], *inv_loads[1], coup_loads[1]):
        load.start()
    stores = [pltpu.make_async_copy(fwd[b], fwd_hbm.at[b], sems.at[8 + b]) for b in range(2)]
    for b in range(2):
        sens_loads[b].wait()
        turned[b] = sens[b].T
        for load, s in zip(inv_loads[b], columns):
            load.wait()
            fwd[b][:, s] = dot(turned[b], inv[b, :, s]).astype(BF16)
        stores[b].start()
        coup_loads[b].wait()
        if b == 0:
            term[...] = dot(fwd0[...], coup0[...])
            part[...] = term[lanes(core, half), :]
    away[...] = (term[lanes(1 - core, half), :] + dot(fwd1[lanes(1 - core, half), :], coup1[...])).astype(BF16)
    for store in stores:
        store.wait()


def mine_kernel(part, fwd1, coup1, out):
    out[...] = part[...] + dot(fwd1[lanes(lax.axis_index("core"), out.shape[0]), :], coup1[...])


def order_kernel(ring0, ring1, ring2, ring3, out):
    yed = lax.axis_index("y")
    for step, ring in enumerate((ring0, ring1, ring2, ring3)):
        out[lax.rem(yed + 4 - step, 4)] = ring[...]


def join_kernel(mine, came, out_hbm, out, sems):
    quarter = out.shape[2]
    copies = []
    for z in range(4):
        span = slice(z * quarter, (z + 1) * quarter)
        value = (mine[:, span] + came[:, span].astype(F32)).astype(BF16)
        out[z * 16:(z + 1) * 16] = value.reshape(16, -1, quarter)
        copies.append(pltpu.make_async_copy(out.at[z * 16:(z + 1) * 16], out_hbm.at[z * 16:(z + 1) * 16], sems.at[z]))
        copies[-1].start()
    for copy in copies:
        copy.wait()


def unroll(got, lhs, side):
    half, quarter = lhs.shape[0] // 2, got.shape[2]
    for z in range(4):
        lhs[lanes(side, half), ORDER[z] * quarter:(ORDER[z] + 1) * quarter] = got[z * 16:(z + 1) * 16].reshape(-1, quarter)


def own_kernel(got, coup_hbm, inv_hbm, pulled, coup, inv, lhs, total, sems):
    third = coup.shape[0] // 3
    half = pulled.shape[0]
    core = lax.axis_index("core")
    spans = [slice(i * third, (i + 1) * third) for i in range(3)]
    loads = [pltpu.make_async_copy(coup_hbm.at[0, s, :], coup.at[s, :], sems.at[i]) for i, s in enumerate(spans)]
    loads.append(pltpu.make_async_copy(inv_hbm.at[0], inv, sems.at[3]))
    for load in loads:
        load.start()
    unroll(got, lhs, core)
    for i, s in enumerate(spans):
        loads[i].wait()
        value = dot(lhs[lanes(core, half), s], coup[s, :])
        total[...] = value if i == 0 else total[...] + value
    pulled[...] = total[...].astype(BF16)
    loads[3].wait()


def other_kernel(
    own, other, pulled_own, coup0, inv0, coup_hbm, inv_hbm, fwd_hbm, adjoint_hbm, border_hbm,
    coup1, inv1, fwd, adjoint, border, lhs, pulled, total, sems,
):
    half, quarter = pulled_own.shape[0], own.shape[2]
    third = coup1.shape[0] // 3
    core = lax.axis_index("core")
    zed = lax.axis_index("z")
    spans = [slice(i * third, (i + 1) * third) for i in range(3)]
    fwd_loads = [pltpu.make_async_copy(fwd_hbm.at[b], fwd.at[b], sems.at[b]) for b in range(2)]
    coup_loads = [pltpu.make_async_copy(coup_hbm.at[1, s, :], coup1.at[s, :], sems.at[2 + i]) for i, s in enumerate(spans)]
    inv_load = pltpu.make_async_copy(inv_hbm.at[1], inv1, sems.at[5])
    for load in (fwd_loads[0], *coup_loads, inv_load, fwd_loads[1]):
        load.start()
    unroll(own, lhs, core)
    unroll(other, lhs, 1 - core)
    pulled[0, lanes(core, half), :] = pulled_own[...]
    pulled[0, lanes(1 - core, half), :] = dot(lhs[lanes(1 - core, half), :], coup0[...]).astype(BF16)

    rows = border.shape[0]
    first = (lax.axis_index("y") * 2 + core) * rows
    spot = first + lax.broadcasted_iota(jnp.int32, (rows, quarter), 0)
    pick = (lax.broadcasted_iota(jnp.int32, (rows, quarter), 1) == spot).astype(BF16)
    source = jnp.where(zed == 0, 0, jnp.where(zed == 1, 3, zed - 1))
    for ref, side in ((own, core), (other, 1 - core)):
        chosen = ref[pl.ds(source * 16, 16)].reshape(-1, quarter)
        picked = lax.dot_general(pick, chosen, (((1,), (1,)), ((), ())), preferred_element_type=F32)
        border[:, lanes(side, half)] = picked.astype(BF16)
    stores = [pltpu.make_async_copy(border, border_hbm, sems.at[6])]
    stores[0].start()

    step = inv1.shape[1] // 4

    def finish(b, inv):
        for i in range(4):
            span = slice(i * step, (i + 1) * step)
            value = fwd[b, :, span].astype(F32) - dot(pulled[b], inv[:, span])
            adjoint[b, span, :] = value.astype(BF16).T
            stores.append(pltpu.make_async_copy(adjoint.at[b, span, :], adjoint_hbm.at[b, span, :], sems.at[7 + 4 * b + i]))
            stores[-1].start()

    fwd_loads[0].wait()
    finish(0, inv0)
    for i, s in enumerate(spans):
        coup_loads[i].wait()
        value = dot(lhs[:, s], coup1[s, :])
        total[...] = value if i == 0 else total[...] + value
    pulled[1] = total[...].astype(BF16)
    inv_load.wait()
    fwd_loads[1].wait()
    finish(1, inv1)
    for store in stores:
        store.wait()


def rhs_kernel(rhs_hbm, out, rhs, sem):
    piece, quarter = out.shape
    cols = rhs.shape[1]
    load = pltpu.make_async_copy(rhs_hbm.at[lanes(lax.axis_index("z"), quarter), :], rhs, sem)
    load.start()
    start = lax.axis_index("core") * (cols // 2) + lax.axis_index(("y", "xh", "xl")) * piece
    spot = start + lax.broadcasted_iota(jnp.int32, (piece, cols), 0)
    pick = (lax.broadcasted_iota(jnp.int32, (piece, cols), 1) == spot).astype(BF16)
    load.wait()
    out[...] = lax.dot_general(pick, rhs[...], (((1,), (1,)), ((), ())), preferred_element_type=F32)


def share_kernel(parts, rhs, plane, keep, give):
    zed = lax.axis_index("z")
    residual = (rhs[...] - jnp.sum(parts[...].astype(F32), axis=0)).astype(BF16)
    share = dot(residual, plane[...])
    half = keep.shape[1]
    inner = (zed == 1) | (zed == 2)
    keep[...] = jnp.where(inner, share[:, half:], share[:, :half])
    give[...] = jnp.where(inner, share[:, :half], share[:, half:])


def steps(block_inverse, coupling_in, coupling_out, sensitivities, border_rhs, border_inverse):
    core = lax.axis_index("core")
    zed = lax.axis_index("z")
    rows, link = border_inverse.shape
    n, cols = sensitivities.shape[1:]
    half, quarter = cols // 2, link // 4
    piece = cols // 32
    sem = pltpu.SemaphoreType.DMA

    ring = [border_inverse]
    for step in (1, 2, 3):
        ring.append(lax.ppermute(border_inverse, "y", [(i, (i + step) % 4) for i in range(4)]))
    ring, = call(order_kernel, (pltpu.VMEM((4, rows, link), BF16),), [VMEM] * 4, ring, (), 2)
    other = lax.ppermute(ring, "core", SWAP)
    plane = jnp.where(core == 0, jnp.stack([ring, other], 1), jnp.stack([other, ring], 1)).reshape(quarter, link)

    fwd, fwd1, away, part, coup1 = call(
        forward_kernel,
        (
            pltpu.HBM((2, cols, n), BF16), pltpu.VMEM((cols, n), BF16), pltpu.VMEM((half, link), BF16),
            pltpu.VMEM((half, link), F32), pltpu.VMEM((n, link), BF16),
        ),
        [HBM] * 3, (sensitivities, block_inverse, coupling_in),
        [
            pltpu.VMEM((2, n, n), BF16), pltpu.VMEM((2, n, cols), BF16), pltpu.VMEM((2, cols, n), BF16), pltpu.VMEM((n, link), BF16),
            pltpu.VMEM((cols, n), BF16), pltpu.VMEM((cols, link), F32), sem((10,)),
        ],
        28, 4 * n * cols * (n + link), 17)
    came = lax.ppermute(away, "core", SWAP)
    mine, = call(mine_kernel, (pltpu.VMEM((half, link), F32),), [VMEM] * 3, (part, fwd1, coup1), (), 8, 2 * n * half * link, 7)
    terms, = call(
        join_kernel, (pltpu.HBM((64, piece, quarter), BF16),), [VMEM] * 2, (mine, came),
        [pltpu.VMEM((64, piece, quarter), BF16), sem((4,))], 4, 0, 3)
    parts = lax.all_to_all(terms, CHIPS, 0, 0, tiled=True)
    rhs, = call(
        rhs_kernel, (pltpu.VMEM((piece, quarter), F32),), [HBM], (border_rhs,),
        [pltpu.VMEM((quarter, cols), BF16), pltpu.SemaphoreType.DMA], 2)
    keep, give = call(
        share_kernel, (pltpu.VMEM((piece, 2 * quarter), F32),) * 2, [VMEM] * 3, (parts, rhs, plane), (), 4)
    share = keep + lax.ppermute(give, "z", NEAR)
    outer = zed // 2
    came = lax.ppermute(lax.dynamic_slice_in_dim(share, (1 - outer) * quarter, quarter, 1), "z", FAR)
    solved = (lax.dynamic_slice_in_dim(share, outer * quarter, quarter, 1) + came).astype(BF16)

    spread = jnp.broadcast_to(solved[None], (64,) + solved.shape)
    own = lax.all_to_all(spread, CHIPS, 0, 0, tiled=True)
    other = lax.ppermute(own, "core", SWAP)

    pulled, coup0, inv0 = call(
        own_kernel, (pltpu.VMEM((half, n), BF16), pltpu.VMEM((link, n), BF16), pltpu.VMEM((n, n), BF16)),
        [VMEM] + [HBM] * 2, (own, coupling_out, block_inverse),
        [pltpu.VMEM((cols, link), BF16), pltpu.VMEM((half, n), F32), sem((4,))], 8, 2 * half * n * link, 6)
    return call(
        other_kernel, (pltpu.HBM((2, n, cols), BF16), pltpu.HBM((rows, cols), BF16)), [VMEM] * 5 + [HBM] * 3,
        (own, other, pulled, coup0, inv0, coupling_out, block_inverse, fwd),
        [
            pltpu.VMEM((link, n), BF16), pltpu.VMEM((n, n), BF16), pltpu.VMEM((2, cols, n), BF16), pltpu.VMEM((2, n, cols), BF16),
            pltpu.VMEM((rows, cols), BF16), pltpu.VMEM((cols, link), BF16), pltpu.VMEM((2, cols, n), BF16), pltpu.VMEM((cols, n), F32), sem((15,)),
        ],
        24, 4 * cols * n * (n + link // 2), 16)


def body(*args):
    return tuple(steps(*args))


def solution(mesh):
    mesh = Mesh(mesh.devices.reshape(4, 4, 2, 2, 2), ("z", "y", "core", "xh", "xl"))
    every = ("z", "y", "core", "xh", "xl")
    blocks = P(every, None, None)
    lines = P(("z", "y", "core"), None)
    return jax.shard_map(
        body, mesh=mesh, in_specs=(blocks, blocks, blocks, blocks, P(), lines), out_specs=(blocks, lines), check_vma=False
    )
```

```python
import jax
import jax.numpy as jnp
from jax import lax
from jax.experimental import pallas as pl
from jax.experimental.pallas import tpu as pltpu
from jax.sharding import Mesh, PartitionSpec as P

F32 = jnp.float32
BF16 = jnp.bfloat16
CHIPS = ("z", "y", "xh", "xl")
SWAP = [(0, 1), (1, 0)]
NEAR = [(0, 1), (1, 0), (2, 3), (3, 2)]
FAR = [(0, 3), (3, 0), (1, 2), (2, 1)]
ORDER = (0, 2, 3, 1)
HBM = pl.BlockSpec(memory_space=pltpu.HBM)
VMEM = pl.BlockSpec(memory_space=pltpu.VMEM)


def call(kernel, outs, ins, operands, scratch=(), mib=16, flops=0, mbytes=1, alias={}):
    return pl.pallas_call(
        kernel,
        out_shape=outs,
        in_specs=ins,
        out_specs=[VMEM if str(o.memory_space) == "vmem" else HBM for o in outs],
        scratch_shapes=list(scratch),
        input_output_aliases=alias,
        compiler_params=pltpu.CompilerParams(vmem_limit_bytes=mib << 20),
        cost_estimate=pl.CostEstimate(flops=flops, bytes_accessed=mbytes << 20, transcendentals=0),
    )(*[pltpu.with_memory_space_constraint(x, s.memory_space) for x, s in zip(operands, ins)])


def dot(a, b):
    return jnp.dot(a, b, preferred_element_type=F32)


def long_dot(a, b):
    cut = b.shape[0] * 2 // 3
    return dot(a[:, :cut], b[:cut]) + dot(a[:, cut:], b[cut:])


def lanes(index, size):
    return pl.ds(pl.multiple_of(index * size, 128), size)


def forward_kernel(sens_hbm, inv_hbm, coup_hbm, fwd_hbm, fwd1, away, term, coup1, inv, sens, turned, coup0, fwd0, sems):
    half = away.shape[0]
    core = lax.axis_index("core")
    fwd, coup = (fwd0, fwd1), (coup0, coup1)
    sens_loads = [pltpu.make_async_copy(sens_hbm.at[b], sens.at[b], sems.at[b]) for b in range(2)]
    inv_loads = [pltpu.make_async_copy(inv_hbm.at[b], inv.at[b], sems.at[2 + b]) for b in range(2)]
    coup_loads = [pltpu.make_async_copy(coup_hbm.at[b], coup[b], sems.at[4 + b]) for b in range(2)]
    for load in (sens_loads[0], inv_loads[0], sens_loads[1], coup_loads[0], inv_loads[1], coup_loads[1]):
        load.start()
    stores = [pltpu.make_async_copy(fwd[b], fwd_hbm.at[b], sems.at[6 + b]) for b in range(2)]
    sens_loads[0].wait()
    turned[0] = sens[0].T
    inv_loads[0].wait()
    sens_loads[1].wait()
    fwd0[...] = dot(turned[0], inv[0]).astype(BF16)
    turned[1] = sens[1].T
    coup_loads[0].wait()
    term[...] = dot(fwd0[...], coup0[...])
    inv_loads[1].wait()
    stores[0].start()
    fwd1[...] = dot(turned[1], inv[1]).astype(BF16)
    coup_loads[1].wait()
    stores[1].start()
    away[...] = (term[lanes(1 - core, half), :] + dot(fwd1[lanes(1 - core, half), :], coup1[...])).astype(BF16)
    for store in stores:
        store.wait()


def mine_kernel(term, fwd1, coup1, out):
    rows = lanes(lax.axis_index("core"), out.shape[0])
    out[...] = term[rows, :] + dot(fwd1[rows, :], coup1[...])


def order_kernel(ring0, ring1, ring2, ring3, out):
    yed = lax.axis_index("y")
    for step, ring in enumerate((ring0, ring1, ring2, ring3)):
        out[lax.rem(yed + 4 - step, 4)] = ring[...]


def join_kernel(mine, came, out):
    quarter = out.shape[2]
    for z in range(4):
        span = slice(z * quarter, (z + 1) * quarter)
        value = (mine[:, span] + came[:, span].astype(F32)).astype(BF16)
        out[z * 16:(z + 1) * 16] = value.reshape(16, -1, quarter)


def unroll(got, lhs, side):
    half, quarter = lhs.shape[0] // 2, got.shape[2]
    for z in range(4):
        lhs[lanes(side, half), ORDER[z] * quarter:(ORDER[z] + 1) * quarter] = got[z * 16:(z + 1) * 16].reshape(-1, quarter)


def own_kernel(got, coup_hbm, inv_hbm, pulled, coup, inv, lhs, total, sems):
    third = coup.shape[0] // 3
    half = pulled.shape[0]
    core = lax.axis_index("core")
    spans = [slice(i * third, (i + 1) * third) for i in range(3)]
    loads = [pltpu.make_async_copy(coup_hbm.at[0, s, :], coup.at[s, :], sems.at[i]) for i, s in enumerate(spans)]
    loads.append(pltpu.make_async_copy(inv_hbm.at[0], inv, sems.at[3]))
    for load in loads:
        load.start()
    unroll(got, lhs, core)
    for i, s in enumerate(spans):
        loads[i].wait()
        value = dot(lhs[lanes(core, half), s], coup[s, :])
        total[...] = value if i == 0 else total[...] + value
    pulled[...] = total[...].astype(BF16)
    loads[3].wait()


def other_kernel(
    own, other, pulled_own, coup0, inv0, coup_hbm, inv_hbm, fwd_hbm, adjoint_hbm, border_hbm,
    coup1, inv1, fwd, adjoint, border, lhs, pulled, value, sems,
):
    half, quarter = pulled_own.shape[0], own.shape[2]
    core = lax.axis_index("core")
    zed = lax.axis_index("z")
    fwd_loads = [pltpu.make_async_copy(fwd_hbm.at[b], fwd.at[b], sems.at[b]) for b in range(2)]
    coup_load = pltpu.make_async_copy(coup_hbm.at[1], coup1, sems.at[2])
    inv_load = pltpu.make_async_copy(inv_hbm.at[1], inv1, sems.at[3])
    for load in (fwd_loads[0], coup_load, inv_load, fwd_loads[1]):
        load.start()
    step = inv1.shape[1] // 4
    spans = [slice(i * step, (i + 1) * step) for i in range(4)]
    stores = []

    def store(b, i):
        stores.append(pltpu.make_async_copy(adjoint.at[b, spans[i], :], adjoint_hbm.at[b, spans[i], :], sems.at[5 + 4 * b + i]))
        stores[-1].start()

    unroll(own, lhs, core)
    unroll(other, lhs, 1 - core)
    pulled[0, lanes(core, half), :] = pulled_own[...]
    pulled[0, lanes(1 - core, half), :] = long_dot(lhs[lanes(1 - core, half), :], coup0).astype(BF16)
    fwd_loads[0].wait()
    for i in range(2):
        s = slice(2 * i * step, 2 * (i + 1) * step)
        value[:, s] = (fwd[0, :, s].astype(F32) - dot(pulled[0], inv0[:, s])).astype(BF16)

    rows = border.shape[0]
    first = (lax.axis_index("y") * 2 + core) * rows
    spot = first + lax.broadcasted_iota(jnp.int32, (rows, quarter), 0)
    pick = (lax.broadcasted_iota(jnp.int32, (rows, quarter), 1) == spot).astype(BF16)
    source = jnp.where(zed == 0, 0, jnp.where(zed == 1, 3, zed - 1))
    coup_load.wait()
    for ref, side in ((own, core), (other, 1 - core)):
        chosen = ref[pl.ds(source * 16, 16)].reshape(-1, quarter)
        picked = lax.dot_general(pick, chosen, (((1,), (1,)), ((), ())), preferred_element_type=F32)
        border[:, lanes(side, half)] = picked.astype(BF16)
    for s in spans:
        adjoint[0, s, :] = value[:, s].T
    pulled[1] = long_dot(lhs, coup1).astype(BF16)
    stores.append(pltpu.make_async_copy(border, border_hbm, sems.at[4]))
    stores[0].start()
    for i in range(4):
        store(0, i)
    inv_load.wait()
    fwd_loads[1].wait()
    for i, s in enumerate(spans):
        for rows in (slice(0, half), slice(half, 2 * half)) if i > 1 else (slice(0, 2 * half),):
            adjoint[1, s, rows] = (fwd[1, rows, s].astype(F32) - dot(pulled[1, rows, :], inv1[:, s])).astype(BF16).T
        store(1, i)
    for copy in stores:
        copy.wait()


def rhs_kernel(rhs_hbm, out, rhs, sem):
    piece, quarter = out.shape
    cols = rhs.shape[1]
    load = pltpu.make_async_copy(rhs_hbm.at[lanes(lax.axis_index("z"), quarter), :], rhs, sem)
    load.start()
    start = lax.axis_index("core") * (cols // 2) + lax.axis_index(("y", "xh", "xl")) * piece
    spot = start + lax.broadcasted_iota(jnp.int32, (piece, cols), 0)
    pick = (lax.broadcasted_iota(jnp.int32, (piece, cols), 1) == spot).astype(BF16)
    load.wait()
    out[...] = lax.dot_general(pick, rhs[...], (((1,), (1,)), ((), ())), preferred_element_type=F32)


def share_kernel(parts, rhs, plane, keep, give):
    zed = lax.axis_index("z")
    residual = (rhs[...] - jnp.sum(parts[...].astype(F32), axis=0)).astype(BF16)
    share = dot(residual, plane[...])
    half = keep.shape[1]
    inner = (zed == 1) | (zed == 2)
    keep[...] = jnp.where(inner, share[:, half:], share[:, :half])
    give[...] = jnp.where(inner, share[:, :half], share[:, half:])


def steps(block_inverse, coupling_in, coupling_out, sensitivities, border_rhs, border_inverse):
    core = lax.axis_index("core")
    zed = lax.axis_index("z")
    rows, link = border_inverse.shape
    n, cols = sensitivities.shape[1:]
    half, quarter = cols // 2, link // 4
    piece = cols // 32
    sem = pltpu.SemaphoreType.DMA

    ring = [border_inverse]
    for step in (1, 2, 3):
        ring.append(lax.ppermute(border_inverse, "y", [(i, (i + step) % 4) for i in range(4)]))
    ring, = call(order_kernel, (pltpu.VMEM((4, rows, link), BF16),), [VMEM] * 4, ring, (), 2)
    other = lax.ppermute(ring, "core", SWAP)
    plane = jnp.where(core == 0, jnp.stack([ring, other], 1), jnp.stack([other, ring], 1)).reshape(quarter, link)

    fwd, fwd1, away, term, coup1 = call(
        forward_kernel,
        (
            pltpu.HBM((2, cols, n), BF16), pltpu.VMEM((cols, n), BF16), pltpu.VMEM((half, link), BF16),
            pltpu.VMEM((cols, link), F32), pltpu.VMEM((n, link), BF16),
        ),
        [HBM] * 3, (sensitivities, block_inverse, coupling_in),
        [
            pltpu.VMEM((2, n, n), BF16), pltpu.VMEM((2, n, cols), BF16), pltpu.VMEM((2, cols, n), BF16), pltpu.VMEM((n, link), BF16),
            pltpu.VMEM((cols, n), BF16), sem((8,)),
        ],
        24, 4 * n * cols * (n + link), 17)
    came = lax.ppermute(away, "core", SWAP)
    mine, = call(mine_kernel, (pltpu.VMEM((half, link), F32),), [VMEM] * 3, (term, fwd1, coup1), (), 8, 2 * n * half * link, 7)
    terms, = call(join_kernel, (pltpu.VMEM((64, piece, quarter), BF16),), [VMEM] * 2, (mine, came), (), 4, 0, 3)
    parts = lax.all_to_all(terms, CHIPS, 0, 0, tiled=True)
    rhs, = call(
        rhs_kernel, (pltpu.VMEM((piece, quarter), F32),), [HBM], (border_rhs,),
        [pltpu.VMEM((quarter, cols), BF16), pltpu.SemaphoreType.DMA], 2)
    keep, give = call(
        share_kernel, (pltpu.VMEM((piece, 2 * quarter), F32),) * 2, [VMEM] * 3, (parts, rhs, plane), (), 4)
    share = keep + lax.ppermute(give, "z", NEAR)
    outer = zed // 2
    came = lax.ppermute(lax.dynamic_slice_in_dim(share, (1 - outer) * quarter, quarter, 1), "z", FAR)
    solved = (lax.dynamic_slice_in_dim(share, outer * quarter, quarter, 1) + came).astype(BF16)

    spread = jnp.broadcast_to(solved[None], (64,) + solved.shape)
    own = lax.all_to_all(spread, CHIPS, 0, 0, tiled=True)
    other = lax.ppermute(own, "core", SWAP)

    pulled, coup0, inv0 = call(
        own_kernel, (pltpu.VMEM((half, n), BF16), pltpu.VMEM((link, n), BF16), pltpu.VMEM((n, n), BF16)),
        [VMEM] + [HBM] * 2, (own, coupling_out, block_inverse),
        [pltpu.VMEM((cols, link), BF16), pltpu.VMEM((half, n), F32), sem((4,))], 8, 2 * half * n * link, 6)
    return call(
        other_kernel, (pltpu.HBM((2, n, cols), BF16), pltpu.HBM((rows, cols), BF16)), [VMEM] * 5 + [HBM] * 3,
        (own, other, pulled, coup0, inv0, coupling_out, block_inverse, fwd),
        [
            pltpu.VMEM((link, n), BF16), pltpu.VMEM((n, n), BF16), pltpu.VMEM((2, cols, n), BF16), pltpu.VMEM((2, n, cols), BF16),
            pltpu.VMEM((rows, cols), BF16), pltpu.VMEM((cols, link), BF16), pltpu.VMEM((2, cols, n), BF16), pltpu.VMEM((cols, n), BF16), sem((13,)),
        ],
        24, 4 * cols * n * (n + link // 2), 16)


def body(*args):
    return tuple(steps(*args))


def solution(mesh):
    mesh = Mesh(mesh.devices.reshape(4, 4, 2, 2, 2), ("z", "y", "core", "xh", "xl"))
    every = ("z", "y", "core", "xh", "xl")
    blocks = P(every, None, None)
    lines = P(("z", "y", "core"), None)
    return jax.shard_map(
        body, mesh=mesh, in_specs=(blocks, blocks, blocks, blocks, P(), lines), out_specs=(blocks, lines), check_vma=False
    )
```

```python
import jax
import jax.numpy as jnp
from jax import lax
from jax.experimental import pallas as pl
from jax.experimental.pallas import tpu as pltpu
from jax.sharding import Mesh, PartitionSpec as P

F32 = jnp.float32
BF16 = jnp.bfloat16
CHIPS = ("z", "y", "xh", "xl")
SWAP = [(0, 1), (1, 0)]
NEAR = [(0, 1), (1, 0), (2, 3), (3, 2)]
FAR = [(0, 3), (3, 0), (1, 2), (2, 1)]
ORDER = (0, 2, 3, 1)
HBM = pl.BlockSpec(memory_space=pltpu.HBM)
VMEM = pl.BlockSpec(memory_space=pltpu.VMEM)


def call(kernel, outs, ins, operands, scratch=(), mib=16, flops=0, mbytes=1, alias={}):
    return pl.pallas_call(
        kernel,
        out_shape=outs,
        in_specs=ins,
        out_specs=[VMEM if str(o.memory_space) == "vmem" else HBM for o in outs],
        scratch_shapes=list(scratch),
        input_output_aliases=alias,
        compiler_params=pltpu.CompilerParams(vmem_limit_bytes=mib << 20),
        cost_estimate=pl.CostEstimate(flops=flops, bytes_accessed=mbytes << 20, transcendentals=0),
    )(*[pltpu.with_memory_space_constraint(x, s.memory_space) for x, s in zip(operands, ins)])


def dot(a, b):
    return jnp.dot(a, b, preferred_element_type=F32)


def long_dot(a, b):
    cut = b.shape[0] * 2 // 3
    return dot(a[:, :cut], b[:cut]) + dot(a[:, cut:], b[cut:])


def lanes(index, size):
    return pl.ds(pl.multiple_of(index * size, 128), size)


def forward_kernel(sens_hbm, inv_hbm, coup_hbm, fwd_hbm, fwd, away, coup0, coup1, inv, sens, turned, total, sems):
    half = away.shape[0]
    cut = coup1.shape[0] // 2
    core = lax.axis_index("core")
    far = lanes(1 - core, half)
    sens_loads = [pltpu.make_async_copy(sens_hbm.at[b], sens.at[b], sems.at[b]) for b in range(2)]
    inv_loads = [pltpu.make_async_copy(inv_hbm.at[b], inv.at[b], sems.at[2 + b]) for b in range(2)]
    coup_load = pltpu.make_async_copy(coup_hbm.at[0], coup0, sems.at[4])
    spans = [slice(0, cut), slice(cut, 2 * cut)]
    last_loads = [pltpu.make_async_copy(coup_hbm.at[1, s, :], coup1.at[s, :], sems.at[5 + i]) for i, s in enumerate(spans)]
    for load in (sens_loads[0], inv_loads[0], sens_loads[1], coup_load, inv_loads[1], *last_loads):
        load.start()
    stores = [pltpu.make_async_copy(fwd.at[b], fwd_hbm.at[b], sems.at[7 + b]) for b in range(2)]
    sens_loads[0].wait()
    turned[0] = sens[0].T
    inv_loads[0].wait()
    sens_loads[1].wait()
    fwd[0] = dot(turned[0], inv[0]).astype(BF16)
    turned[1] = sens[1].T
    coup_load.wait()
    total[...] = dot(fwd[0, far, :], coup0[...])
    inv_loads[1].wait()
    stores[0].start()
    fwd[1] = dot(turned[1], inv[1]).astype(BF16)
    last_loads[0].wait()
    stores[1].start()
    total[...] += dot(fwd[1, far, spans[0]], coup1[spans[0], :])
    last_loads[1].wait()
    away[...] = (total[...] + dot(fwd[1, far, spans[1]], coup1[spans[1], :])).astype(BF16)
    for store in stores:
        store.wait()


def mine_kernel(fwd, coup0, coup1, out):
    rows = lanes(lax.axis_index("core"), out.shape[0])
    out[...] = dot(fwd[0, rows, :], coup0[...]) + dot(fwd[1, rows, :], coup1[...])


def order_kernel(ring0, ring1, ring2, ring3, out):
    yed = lax.axis_index("y")
    for step, ring in enumerate((ring0, ring1, ring2, ring3)):
        out[lax.rem(yed + 4 - step, 4)] = ring[...]


def join_kernel(mine, came, out):
    quarter = out.shape[2]
    for z in range(4):
        span = slice(z * quarter, (z + 1) * quarter)
        value = (mine[:, span] + came[:, span].astype(F32)).astype(BF16)
        out[z * 16:(z + 1) * 16] = value.reshape(16, -1, quarter)


def unroll(got, lhs, side):
    half, quarter = lhs.shape[0] // 2, got.shape[2]
    for z in range(4):
        lhs[lanes(side, half), ORDER[z] * quarter:(ORDER[z] + 1) * quarter] = got[z * 16:(z + 1) * 16].reshape(-1, quarter)


def own_kernel(got, coup_hbm, inv_hbm, pulled, coup, inv, lhs, total, sems):
    third = coup.shape[0] // 3
    half = pulled.shape[0]
    core = lax.axis_index("core")
    spans = [slice(i * third, (i + 1) * third) for i in range(3)]
    loads = [pltpu.make_async_copy(coup_hbm.at[0, s, :], coup.at[s, :], sems.at[i]) for i, s in enumerate(spans)]
    loads.append(pltpu.make_async_copy(inv_hbm.at[0], inv, sems.at[3]))
    for load in loads:
        load.start()
    unroll(got, lhs, core)
    for i, s in enumerate(spans):
        loads[i].wait()
        value = dot(lhs[lanes(core, half), s], coup[s, :])
        total[...] = value if i == 0 else total[...] + value
    pulled[...] = total[...].astype(BF16)
    loads[3].wait()


def other_kernel(
    own, other, pulled_own, coup0, inv0, coup_hbm, inv_hbm, fwd_hbm, adjoint_hbm, border_hbm,
    coup1, inv1, fwd, adjoint, border, lhs, pulled, value, sems,
):
    half, quarter = pulled_own.shape[0], own.shape[2]
    core = lax.axis_index("core")
    zed = lax.axis_index("z")
    fwd_loads = [pltpu.make_async_copy(fwd_hbm.at[b], fwd.at[b], sems.at[b]) for b in range(2)]
    coup_load = pltpu.make_async_copy(coup_hbm.at[1], coup1, sems.at[2])
    inv_load = pltpu.make_async_copy(inv_hbm.at[1], inv1, sems.at[3])
    for load in (fwd_loads[0], coup_load, inv_load, fwd_loads[1]):
        load.start()
    step = inv1.shape[1] // 4
    spans = [slice(i * step, (i + 1) * step) for i in range(4)]
    stores = []

    def store(b, i):
        stores.append(pltpu.make_async_copy(adjoint.at[b, spans[i], :], adjoint_hbm.at[b, spans[i], :], sems.at[5 + 4 * b + i]))
        stores[-1].start()

    unroll(own, lhs, core)
    unroll(other, lhs, 1 - core)
    pulled[0, lanes(core, half), :] = pulled_own[...]
    pulled[0, lanes(1 - core, half), :] = long_dot(lhs[lanes(1 - core, half), :], coup0).astype(BF16)
    fwd_loads[0].wait()
    for i in range(2):
        s = slice(2 * i * step, 2 * (i + 1) * step)
        value[:, s] = (fwd[0, :, s].astype(F32) - dot(pulled[0], inv0[:, s])).astype(BF16)

    rows = border.shape[0]
    first = (lax.axis_index("y") * 2 + core) * rows
    spot = first + lax.broadcasted_iota(jnp.int32, (rows, quarter), 0)
    pick = (lax.broadcasted_iota(jnp.int32, (rows, quarter), 1) == spot).astype(BF16)
    source = jnp.where(zed == 0, 0, jnp.where(zed == 1, 3, zed - 1))
    coup_load.wait()
    for ref, side in ((own, core), (other, 1 - core)):
        chosen = ref[pl.ds(source * 16, 16)].reshape(-1, quarter)
        picked = lax.dot_general(pick, chosen, (((1,), (1,)), ((), ())), preferred_element_type=F32)
        border[:, lanes(side, half)] = picked.astype(BF16)
    for s in spans:
        adjoint[0, s, :] = value[:, s].T
    pulled[1] = long_dot(lhs, coup1).astype(BF16)
    stores.append(pltpu.make_async_copy(border, border_hbm, sems.at[4]))
    stores[0].start()
    for i in range(4):
        store(0, i)
    inv_load.wait()
    fwd_loads[1].wait()
    for i, s in enumerate(spans):
        for rows in (slice(0, half), slice(half, 2 * half)) if i > 1 else (slice(0, 2 * half),):
            adjoint[1, s, rows] = (fwd[1, rows, s].astype(F32) - dot(pulled[1, rows, :], inv1[:, s])).astype(BF16).T
        store(1, i)
    for copy in stores:
        copy.wait()


def rhs_kernel(rhs_hbm, out, rhs, sem):
    piece, quarter = out.shape
    cols = rhs.shape[1]
    load = pltpu.make_async_copy(rhs_hbm.at[lanes(lax.axis_index("z"), quarter), :], rhs, sem)
    load.start()
    start = lax.axis_index("core") * (cols // 2) + lax.axis_index(("y", "xh", "xl")) * piece
    spot = start + lax.broadcasted_iota(jnp.int32, (piece, cols), 0)
    pick = (lax.broadcasted_iota(jnp.int32, (piece, cols), 1) == spot).astype(BF16)
    load.wait()
    out[...] = lax.dot_general(pick, rhs[...], (((1,), (1,)), ((), ())), preferred_element_type=F32)


def share_kernel(parts, rhs, plane, keep, give):
    zed = lax.axis_index("z")
    residual = (rhs[...] - jnp.sum(parts[...].astype(F32), axis=0)).astype(BF16)
    share = dot(residual, plane[...])
    half = keep.shape[1]
    inner = (zed == 1) | (zed == 2)
    keep[...] = jnp.where(inner, share[:, half:], share[:, :half])
    give[...] = jnp.where(inner, share[:, :half], share[:, half:])


def steps(block_inverse, coupling_in, coupling_out, sensitivities, border_rhs, border_inverse):
    core = lax.axis_index("core")
    zed = lax.axis_index("z")
    rows, link = border_inverse.shape
    n, cols = sensitivities.shape[1:]
    half, quarter = cols // 2, link // 4
    piece = cols // 32
    sem = pltpu.SemaphoreType.DMA

    ring = [border_inverse]
    for step in (1, 2, 3):
        ring.append(lax.ppermute(border_inverse, "y", [(i, (i + step) % 4) for i in range(4)]))
    ring, = call(order_kernel, (pltpu.VMEM((4, rows, link), BF16),), [VMEM] * 4, ring, (), 2)
    other = lax.ppermute(ring, "core", SWAP)
    plane = jnp.where(core == 0, jnp.stack([ring, other], 1), jnp.stack([other, ring], 1)).reshape(quarter, link)

    fwd, fwd_near, away, coup0, coup1 = call(
        forward_kernel,
        (pltpu.HBM((2, cols, n), BF16), pltpu.VMEM((2, cols, n), BF16), pltpu.VMEM((half, link), BF16)) + (pltpu.VMEM((n, link), BF16),) * 2,
        [HBM] * 3, (sensitivities, block_inverse, coupling_in),
        [pltpu.VMEM((2, n, n), BF16), pltpu.VMEM((2, n, cols), BF16), pltpu.VMEM((2, cols, n), BF16), pltpu.VMEM((half, link), F32), sem((9,))],
        24, 4 * n * cols * (n + link // 2), 17)
    came = lax.ppermute(away, "core", SWAP)
    mine, = call(mine_kernel, (pltpu.VMEM((half, link), F32),), [VMEM] * 3, (fwd_near, coup0, coup1), (), 8, 4 * n * half * link, 9)
    terms, = call(join_kernel, (pltpu.VMEM((64, piece, quarter), BF16),), [VMEM] * 2, (mine, came), (), 4, 0, 3)
    parts = lax.all_to_all(terms, CHIPS, 0, 0, tiled=True)
    rhs, = call(
        rhs_kernel, (pltpu.VMEM((piece, quarter), F32),), [HBM], (border_rhs,),
        [pltpu.VMEM((quarter, cols), BF16), pltpu.SemaphoreType.DMA], 2)
    keep, give = call(
        share_kernel, (pltpu.VMEM((piece, 2 * quarter), F32),) * 2, [VMEM] * 3, (parts, rhs, plane), (), 4)
    share = keep + lax.ppermute(give, "z", NEAR)
    outer = zed // 2
    came = lax.ppermute(lax.dynamic_slice_in_dim(share, (1 - outer) * quarter, quarter, 1), "z", FAR)
    solved = (lax.dynamic_slice_in_dim(share, outer * quarter, quarter, 1) + came).astype(BF16)

    spread = jnp.broadcast_to(solved[None], (64,) + solved.shape)
    own = lax.all_to_all(spread, CHIPS, 0, 0, tiled=True)
    other = lax.ppermute(own, "core", SWAP)

    pulled, pull0, inv0 = call(
        own_kernel, (pltpu.VMEM((half, n), BF16), pltpu.VMEM((link, n), BF16), pltpu.VMEM((n, n), BF16)),
        [VMEM] + [HBM] * 2, (own, coupling_out, block_inverse),
        [pltpu.VMEM((cols, link), BF16), pltpu.VMEM((half, n), F32), sem((4,))], 8, 2 * half * n * link, 6)
    return call(
        other_kernel, (pltpu.HBM((2, n, cols), BF16), pltpu.HBM((rows, cols), BF16)), [VMEM] * 5 + [HBM] * 3,
        (own, other, pulled, pull0, inv0, coupling_out, block_inverse, fwd),
        [
            pltpu.VMEM((link, n), BF16), pltpu.VMEM((n, n), BF16), pltpu.VMEM((2, cols, n), BF16), pltpu.VMEM((2, n, cols), BF16),
            pltpu.VMEM((rows, cols), BF16), pltpu.VMEM((cols, link), BF16), pltpu.VMEM((2, cols, n), BF16), pltpu.VMEM((cols, n), BF16), sem((13,)),
        ],
        24, 4 * cols * n * (n + link // 2), 16)


def body(*args):
    return tuple(steps(*args))


def solution(mesh):
    mesh = Mesh(mesh.devices.reshape(4, 4, 2, 2, 2), ("z", "y", "core", "xh", "xl"))
    every = ("z", "y", "core", "xh", "xl")
    blocks = P(every, None, None)
    lines = P(("z", "y", "core"), None)
    return jax.shard_map(
        body, mesh=mesh, in_specs=(blocks, blocks, blocks, blocks, P(), lines), out_specs=(blocks, lines), check_vma=False
    )
```
